32 devices in a mesh: dp: 4 (over z), ctx: 8 (over y, x, core).
Axes of the slice: x: 2, y: 2, z: 4, core: 2. Of those that a mesh axis runs over, the one named last changes fastest.
Arguments:
- inputs: bfloat16 [4, 1024, 1024], P('dp', 'ctx'), may hold values from -6 to 6
- cotangent: bfloat16 [4, 1024, 1024], P('dp', 'ctx'), may hold values from -6 to 6
- mixer_params: float32 [4194304], P(('dp', 'ctx')), may hold values from -0.1875 to 0.1875
- mixer_first: float32 [4194304], P(('dp', 'ctx')), may hold values from -0.0014648438 to 0.0014648438
- mixer_second: float32 [4194304], P(('dp', 'ctx')), may hold values from 2.3434208e-11 to 2.3434207e-10
- ffn_params: float32 [4325376], P(('dp', 'ctx')), may hold values from -0.21320072 to 0.21320072
- ffn_first: float32 [4325376], P(('dp', 'ctx')), may hold values from -0.0014648438 to 0.0014648438
- ffn_second: float32 [4325376], P(('dp', 'ctx')), may hold values from 2.3434208e-11 to 2.3434207e-10
- small_params: float32 [14852], replicated, may hold values from -7 to 2.8
- small_first: float32 [14852], replicated, may hold values from -0.0014648438 to 0.0014648438
- small_second: float32 [14852], replicated, may hold values from 2.3434208e-11 to 2.3434208e-07
Outputs:
- outputs: bfloat16 [4, 1024, 1024], P('dp', 'ctx')
- grad_inputs: bfloat16 [4, 1024, 1024], P('dp', 'ctx')
- mixer_grad: float32 [4194304], P(('dp', 'ctx'))
- ffn_grad: float32 [4325376], P(('dp', 'ctx'))
- small_grad: float32 [14852], replicated
- mixer_new: float32 [4194304], P(('dp', 'ctx'))
- mixer_first_new: float32 [4194304], P(('dp', 'ctx'))
- mixer_second_new: float32 [4194304], P(('dp', 'ctx'))
- ffn_new: float32 [4325376], P(('dp', 'ctx'))
- ffn_first_new: float32 [4325376], P(('dp', 'ctx'))
- ffn_second_new: float32 [4325376], P(('dp', 'ctx'))
- small_new: float32 [14852], replicated
- small_first_new: float32 [14852], replicated
- small_second_new: float32 [14852], replicated
The draws below stay inside these ranges and needn't reach their ends.
All inputs are finite; a program needn't handle non-finite values.
Results may differ from the reference program's by a relative error of at most 0.013.
Values may be sent and summed in bfloat16 or wider, within the bound.
A program may use at most 320 MiB of HBM per device.

```python
import math
import jax
import jax.numpy as jnp
from jax import lax

D = 1024
H = 2
DK = 256
DV = 512
FF = 1408
CONV = 4
GROUP = 64
SEQS = 4
LEN = 1024
ROWS_MIX = 4096
ROWS_FFN = 4224
SMALL = 14852


def draw_mixer_params(key, part):
    total_rows = 2 * H * DK + 3 * H * DV
    row_index = jnp.arange(total_rows)[:, None]
    scales = jnp.where(row_index < 2 * H * DK + 2 * H * DV, D ** (-0.5), 1.5 * (H * DV) ** (-0.5))
    base = jax.random.truncated_normal(key, -4.0, 4.0, (total_rows, D), jnp.float32)
    return (base * scales).reshape(-1)


def draw_ffn_params(key, part):
    total_rows = 3 * FF
    row_index = jnp.arange(total_rows)[:, None]
    scales = jnp.where(row_index < 2 * FF, D ** (-0.5), 2.0 * FF ** (-0.5))
    base = jax.random.truncated_normal(key, -4.0, 4.0, (total_rows, D), jnp.float32)
    return (base * scales).reshape(-1)


def draw_small_params(key, part):
    width = 2 * H * DK + H * DV
    key_list = jax.random.split(key, 5)
    gain_values = 1.0 + 0.1 * jax.random.truncated_normal(key_list[0], -4.0, 4.0, (2 * D + DV,), jnp.float32)
    tap_values = 0.5 * jax.random.truncated_normal(key_list[1], -3.0, 3.0, (CONV * width,), jnp.float32)
    column = jnp.arange(2 * H)
    column_scale = jnp.where(column < H, 1.0, 1.5) * D ** (-0.5)
    gate_weights = jax.random.truncated_normal(key_list[2], -4.0, 4.0, (D, 2 * H), jnp.float32) * column_scale
    a_log = jax.random.uniform(key_list[3], (H,), jnp.float32, 0.0, 2.77)
    log_step = jax.random.uniform(key_list[4], (H,), jnp.float32, jnp.log(0.001), jnp.log(0.1))
    dt_bias = jnp.log(jnp.expm1(jnp.exp(log_step)))
    return jnp.concatenate([gain_values, tap_values, gate_weights.reshape(-1), a_log, dt_bias])


def shard_levels(stream_key, shape, cuts, low, largest):
    level, own = 1.0, jax.random.fold_in(stream_key, 6)
    for dim, blocks in cuts:
        heights = jnp.exp(jax.random.uniform(jax.random.fold_in(own, dim), (blocks,), jnp.float32, low / len(cuts), largest / len(cuts)))
        level = level * jnp.repeat(heights, shape[dim] // blocks).reshape([-1 if axis == dim else 1 for axis in range(len(shape))])
    return level


def noise(rng, extent, deviation, bound, shards=(), kind=jnp.bfloat16):
    values = jax.random.normal(rng, extent, jnp.float32) * deviation
    if len(shards) > 0:
        values = shard_levels(rng, extent, shards, -0.22, 0.18) * values
    return jnp.clip(values, min=-bound, max=bound).astype(kind)


def setup_inputs(seed: int = 0) -> dict:
    splits = jax.random.split(jax.random.key(seed), 12)
    inputs = noise(splits[0], (SEQS, LEN, D), 1.0, 6.0, ((0, 4), (1, 8)))
    cotangent = noise(splits[1], (SEQS, LEN, D), 1.0, 6.0, ((0, 4), (1, 8)))
    mixer_params = draw_mixer_params(jax.random.fold_in(splits[11], 71), 0)
    mixer_first = noise(splits[3], (ROWS_MIX * D,), (0.3 * ((ROWS_MIX + ROWS_FFN) * D + SMALL) ** -0.5), 0.0014648438, ((0, 32),), jnp.float32)
    mixer_second = jnp.clip(jnp.exp(math.log(2.343420735240187e-10) - 2.3025851 * jax.random.uniform(splits[4], (ROWS_MIX * D,), jnp.float32) ** shard_levels(splits[4], (ROWS_MIX * D,), ((0, 32),), -0.2, 0.2)), 2.3434207699346565e-11, 2.343420735240187e-10)
    ffn_params = draw_ffn_params(jax.random.fold_in(splits[11], 71), 0)
    ffn_first = noise(splits[6], (ROWS_FFN * D,), (0.3 * ((ROWS_MIX + ROWS_FFN) * D + SMALL) ** -0.5), 0.0014648438, ((0, 32),), jnp.float32)
    ffn_second = jnp.clip(jnp.exp(math.log(2.343420735240187e-10) - 2.3025851 * jax.random.uniform(splits[7], (ROWS_FFN * D,), jnp.float32) ** shard_levels(splits[7], (ROWS_FFN * D,), ((0, 32),), -0.2, 0.2)), 2.3434207699346565e-11, 2.343420735240187e-10)
    small_params = draw_small_params(jax.random.fold_in(splits[11], 71), 0)
    small_first = noise(splits[9], (SMALL,), (0.3 * ((ROWS_MIX + ROWS_FFN) * D + SMALL) ** -0.5), 0.0014648438, (), jnp.float32)
    small_second = jnp.clip(jnp.exp(jax.random.uniform(splits[10], (SMALL,), jnp.float32, math.log(2.3434207699346565e-11), math.log(2.3434208173966908e-07))), 2.3434207699346565e-11, 2.3434208173966908e-07)
    return {"inputs": inputs, "cotangent": cotangent, "mixer_params": mixer_params, "mixer_first": mixer_first, "mixer_second": mixer_second, "ffn_params": ffn_params, "ffn_first": ffn_first, "ffn_second": ffn_second, "small_params": small_params, "small_first": small_first, "small_second": small_second}


EPSILON = 1e-06
ADAM_EPS = 1e-08
LEARN_RATE = 0.02
BETA_ONE = 0.9
BETA_TWO = 0.999
DECAY_RATE = 0.1
CORRECT_ONE = 1.0 - 0.9 ** 3
CORRECT_TWO = 1.0 - 0.999 ** 3
MAX_NORM = 1.0
HIGHEST = lax.Precision.HIGHEST

def norm_scale(values, gain):
    return values * lax.rsqrt(lax.optimization_barrier(jnp.mean(values * values, axis=-1, keepdims=True)) + EPSILON) * gain

def swiglu(gate_part, up_part):
    return jax.nn.silu(gate_part) * up_part

def unpack_small(packed):
    width = 2 * H * DK + H * DV
    lengths = [D, D, DV, CONV * width, D * 2 * H, H, H]
    pieces = []
    offset = 0
    for length in lengths:
        pieces.append(packed[offset:offset + length])
        offset = offset + length
    return (pieces[0], pieces[1], pieces[2], pieces[3].reshape(CONV, width), pieces[4].reshape(D, 2 * H), pieces[5], pieces[6])

def split_weights(mix_whole, ffn_whole):
    mix_rows = mix_whole.reshape(-1, D)
    ffn_rows = ffn_whole.reshape(-1, D)
    edge = 2 * H * DK + 2 * H * DV
    return (mix_rows[:edge], mix_rows[edge:], ffn_rows[:2 * FF], ffn_rows[2 * FF:])

def features(extended, tap_values, gate_logits, a_log, dt_bias):
    count = extended.shape[0] - (CONV - 1)
    summed = tap_values[0] * extended[0:count]
    for tap_index in range(1, CONV):
        summed = summed + tap_values[tap_index] * extended[tap_index:tap_index + count]
    activated = jax.nn.silu(summed)
    query_part = activated[:, :H * DK].reshape(count, H, DK)
    key_part = activated[:, H * DK:2 * H * DK].reshape(count, H, DK)
    value_part = activated[:, 2 * H * DK:].reshape(count, H, DV)
    query = query_part * lax.rsqrt(lax.optimization_barrier(jnp.sum(query_part * query_part, axis=-1, keepdims=True)) + EPSILON) * DK ** (-0.5)
    keys = key_part * lax.rsqrt(lax.optimization_barrier(jnp.sum(key_part * key_part, axis=-1, keepdims=True)) + EPSILON)
    beta = jax.nn.sigmoid(gate_logits[:, :H])
    decay = -jnp.exp(a_log) * jax.nn.softplus(gate_logits[:, H:] + dt_bias)
    return (jnp.transpose(query, (1, 0, 2)), jnp.transpose(keys, (1, 0, 2)), jnp.transpose(value_part, (1, 0, 2)), beta.T, decay.T)

def split_groups(values):
    blocks = values.shape[1] // GROUP
    shaped = values.reshape((values.shape[0], blocks, GROUP) + values.shape[2:])
    return jnp.moveaxis(shaped, 1, 0)

def group_parts(key_block, value_block, beta_block, decay_block):
    size = decay_block.shape[-1]
    cumulative = jnp.cumsum(decay_block, axis=-1)
    row_index = lax.broadcasted_iota(jnp.int32, (size, size), 0)
    col_index = lax.broadcasted_iota(jnp.int32, (size, size), 1)
    lower = row_index >= col_index
    strict = row_index > col_index
    spread = jnp.where(lower, cumulative[:, :, None] - cumulative[:, None, :], 0.0)
    decay_matrix = jnp.where(lower, jnp.exp(spread), 0.0)
    key_gram = jnp.einsum('hid,hjd->hij', key_block, key_block, precision=HIGHEST)
    system = jnp.where(strict, beta_block[:, :, None] * key_gram * decay_matrix, 0.0) + jnp.eye(size, dtype=key_block.dtype)
    right_side = jnp.concatenate([key_block * (beta_block * jnp.exp(cumulative))[:, :, None], value_block * beta_block[:, :, None]], axis=-1)
    solved = jax.scipy.linalg.solve_triangular(system, right_side, lower=True, unit_diagonal=True)
    key_mix = solved[..., :DK]
    value_mix = solved[..., DK:]
    last_decay = cumulative[:, -1]
    keys_to_end = key_block * jnp.exp(last_decay[:, None] - cumulative)[:, :, None]
    return (cumulative, decay_matrix, key_mix, value_mix, last_decay, keys_to_end)

def group_run(state, pieces):
    query_block, key_block, value_block, beta_block, decay_block = pieces
    cumulative, decay_matrix, key_mix, value_mix, last_decay, keys_to_end = group_parts(key_block, value_block, beta_block, decay_block)
    pseudo_values = value_mix - jnp.einsum('hcd,hde->hce', key_mix, state, precision=HIGHEST)
    scores = jnp.einsum('hid,hjd->hij', query_block, key_block, precision=HIGHEST) * decay_matrix
    block_out = jnp.einsum('hcd,hde->hce', query_block * jnp.exp(cumulative)[:, :, None], state, precision=HIGHEST)
    block_out = block_out + jnp.einsum('hij,hje->hie', scores, pseudo_values, precision=HIGHEST)
    next_state = jnp.exp(last_decay)[:, None, None] * state + jnp.einsum('hcd,hce->hde', keys_to_end, pseudo_values, precision=HIGHEST)
    return (next_state, block_out)

def mixer_run(state, query, keys, values, beta, decay):
    pieces = (split_groups(query), split_groups(keys), split_groups(values), split_groups(beta), split_groups(decay))
    final_state, blocks_out = lax.scan(group_run, state, pieces)
    joined = jnp.moveaxis(blocks_out, 0, 1)
    return (joined.reshape(joined.shape[0], -1, joined.shape[-1]), final_state)

def gated_norm(mixed, out_gate, gain_head):
    count = out_gate.shape[0]
    heads = jnp.transpose(mixed, (1, 0, 2))
    normed = norm_scale(heads, gain_head)
    return (normed * jax.nn.silu(out_gate.reshape(count, H, DV))).reshape(count, H * DV)

def adam_step(weight, grad_full, first, second, clip):
    grad_clipped = grad_full * clip
    first_new = BETA_ONE * first + (1.0 - BETA_ONE) * grad_clipped
    second_new = BETA_TWO * second + (1.0 - BETA_TWO) * grad_clipped * grad_clipped
    update = first_new / CORRECT_ONE / (jnp.sqrt(second_new / CORRECT_TWO) + ADAM_EPS) + DECAY_RATE * weight
    return (weight - LEARN_RATE * update, first_new, second_new)

def sequence_pass(seq_in, seq_grad, weights, parts):
    w_in, w_out, w_ffn, w_down = weights
    gain_one, gain_two, gain_head, tap_values, w_gates, a_log, dt_bias = parts
    width = tap_values.shape[1]
    x_float = seq_in.astype(jnp.float32)
    normed_in = norm_scale(x_float, gain_one).astype(jnp.bfloat16)
    projected = jnp.dot(normed_in.astype(jnp.float32), w_in.T.astype(jnp.float32), preferred_element_type=jnp.float32)
    gate_logits = jnp.dot(normed_in.astype(jnp.float32), w_gates, precision=HIGHEST)
    extended = jnp.concatenate([jnp.zeros((CONV - 1, width), jnp.float32), projected[:, :width]], axis=0)
    out_gate = projected[:, width:]
    query, keys, values, beta, decay = features(extended, tap_values, gate_logits, a_log, dt_bias)
    start = jnp.zeros((H, DK, DV), jnp.float32)
    mixed, final_state = mixer_run(start, query, keys, values, beta, decay)
    head_out = gated_norm(mixed, out_gate, gain_head).astype(jnp.bfloat16)
    resid = x_float + jnp.dot(head_out.astype(jnp.float32), w_out.astype(jnp.float32), preferred_element_type=jnp.float32)
    normed_mid = norm_scale(resid, gain_two).astype(jnp.bfloat16)
    ffn_pre = jnp.dot(normed_mid.astype(jnp.float32), w_ffn.T.astype(jnp.float32), preferred_element_type=jnp.float32)
    gate_part = ffn_pre[:, :FF]
    up_part = ffn_pre[:, FF:]
    hidden_act = swiglu(gate_part, up_part).astype(jnp.bfloat16)
    result = (resid + jnp.dot(hidden_act.astype(jnp.float32), w_down.astype(jnp.float32), preferred_element_type=jnp.float32)).astype(jnp.bfloat16)
    grad_float = seq_grad.astype(jnp.float32)
    grad_down = jnp.dot(hidden_act.T.astype(jnp.float32), seq_grad.astype(jnp.float32), preferred_element_type=jnp.float32)
    grad_hidden = jnp.dot(seq_grad.astype(jnp.float32), w_down.T.astype(jnp.float32), preferred_element_type=jnp.float32)
    unused_one, pull_swiglu = jax.vjp(swiglu, gate_part, up_part)
    grad_gate, grad_up = pull_swiglu(grad_hidden)
    grad_pre = jnp.concatenate([grad_gate, grad_up], axis=1).astype(jnp.bfloat16)
    grad_ffn = jnp.dot(grad_pre.T.astype(jnp.float32), normed_mid.astype(jnp.float32), preferred_element_type=jnp.float32)
    grad_mid = jnp.dot(grad_pre.astype(jnp.float32), w_ffn.astype(jnp.float32), preferred_element_type=jnp.float32)
    unused_two, pull_mid = jax.vjp(norm_scale, resid, gain_two)
    grad_through, grad_gain_two = pull_mid(grad_mid)
    grad_resid = grad_float + grad_through
    resid_half = grad_resid.astype(jnp.bfloat16)
    grad_out = jnp.dot(head_out.T.astype(jnp.float32), resid_half.astype(jnp.float32), preferred_element_type=jnp.float32)
    grad_head = jnp.dot(resid_half.astype(jnp.float32), w_out.T.astype(jnp.float32), preferred_element_type=jnp.float32)
    unused_three, pull_gated = jax.vjp(gated_norm, mixed, out_gate, gain_head)
    grad_mixed, grad_gate_out, grad_gain_head = pull_gated(grad_head)
    unused_four, pull_mixer = jax.vjp(mixer_run, start, query, keys, values, beta, decay)
    mixer_grads = pull_mixer((grad_mixed, jnp.zeros_like(final_state)))
    unused_five, pull_feat = jax.vjp(features, extended, tap_values, gate_logits, a_log, dt_bias)
    grad_ext, grad_taps, grad_logits, grad_alog, grad_bias = pull_feat(mixer_grads[1:])
    grad_proj = jnp.concatenate([grad_ext[CONV - 1:], grad_gate_out], axis=1).astype(jnp.bfloat16)
    grad_in = jnp.dot(grad_proj.T.astype(jnp.float32), normed_in.astype(jnp.float32), preferred_element_type=jnp.float32)
    grad_normed = jnp.dot(grad_proj.astype(jnp.float32), w_in.astype(jnp.float32), preferred_element_type=jnp.float32) + jnp.dot(grad_logits, w_gates.T, precision=HIGHEST)
    grad_gates = jnp.dot(normed_in.astype(jnp.float32).T, grad_logits, precision=HIGHEST)
    unused_six, pull_in = jax.vjp(norm_scale, x_float, gain_one)
    grad_x, grad_gain_one = pull_in(grad_normed)
    grad_input = (grad_resid + grad_x).astype(jnp.bfloat16)
    grad_small = jnp.concatenate([grad_gain_one, grad_gain_two, grad_gain_head, grad_taps.reshape(-1), grad_gates.reshape(-1), grad_alog, grad_bias])
    return (result, grad_input, grad_in, grad_out, grad_ffn, grad_down, grad_small)

def reference(inputs, cotangent, mixer_params, mixer_first, mixer_second, ffn_params, ffn_first, ffn_second, small_params, small_first, small_second):
    weights = split_weights(mixer_params.astype(jnp.bfloat16), ffn_params.astype(jnp.bfloat16))
    parts = unpack_small(small_params)

    def one_sequence(carry, pair):
        seq_in, seq_grad = pair
        result, grad_input, grad_in, grad_out, grad_ffn, grad_down, grad_small = sequence_pass(seq_in, seq_grad, weights, parts)
        updated = (carry[0] + jnp.concatenate([grad_in, grad_out], axis=0), carry[1] + jnp.concatenate([grad_ffn, grad_down], axis=0), carry[2] + grad_small)
        return (updated, (result, grad_input))
    start = (jnp.zeros((2 * H * DK + 3 * H * DV, D), jnp.float32), jnp.zeros((3 * FF, D), jnp.float32), jnp.zeros(small_params.shape, jnp.float32))
    totals, stacked = lax.scan(one_sequence, start, (inputs, cotangent))
    mixer_grad = totals[0].reshape(-1)
    ffn_grad = totals[1].reshape(-1)
    small_grad = totals[2]
    squares = jnp.sum(mixer_grad * mixer_grad) + jnp.sum(ffn_grad * ffn_grad) + jnp.sum(small_grad * small_grad)
    clip = jnp.minimum(1.0, MAX_NORM / (jnp.sqrt(squares) + 1e-06))
    mixer_new, mixer_first_new, mixer_second_new = adam_step(mixer_params, mixer_grad, mixer_first, mixer_second, clip)
    ffn_new, ffn_first_new, ffn_second_new = adam_step(ffn_params, ffn_grad, ffn_first, ffn_second, clip)
    small_new, small_first_new, small_second_new = adam_step(small_params, small_grad, small_first, small_second, clip)
    return (stacked[0], stacked[1], mixer_grad, ffn_grad, small_grad, mixer_new, mixer_first_new, mixer_second_new, ffn_new, ffn_first_new, ffn_second_new, small_new, small_first_new, small_second_new)
```

```python
import math
import jax
import jax.numpy as jnp
from jax import lax
from jax.experimental import pallas as pl
from jax.experimental.pallas import tpu as pltpu
from jax.sharding import PartitionSpec as P

D = 1024
H = 2
DK = 256
DV = 512
FF = 1408
CONV = 4
GROUP = 64


EPSILON = 1e-06
ADAM_EPS = 1e-08
LEARN_RATE = 0.02
BETA_ONE = 0.9
BETA_TWO = 0.999
DECAY_RATE = 0.1
CORRECT_ONE = 1.0 - 0.9**3
CORRECT_TWO = 1.0 - 0.999**3
MAX_NORM = 1.0
HIGHEST = lax.Precision.HIGHEST


def from_behind(value, axis, steps):
    count = lax.axis_size(axis)
    initial, last = (max(0, -steps), min(count, count - steps))
    return lax.ppermute(value, axis, [(source, source + steps) for source in range(initial, last)])


def norm_scale(values, gain):
    return values * lax.rsqrt(jnp.mean(values * values, axis=-1, keepdims=True) + EPSILON) * gain


def swiglu(gate_part, up_part):
    return jax.nn.silu(gate_part) * up_part


def unpack_small(packed):
    width = 2 * H * DK + H * DV
    lengths = [D, D, DV, CONV * width, D * 2 * H, H, H]
    pieces = []
    offset = 0
    for length in lengths:
        pieces.append(packed[offset : offset + length])
        offset = offset + length
    return (
        pieces[0],
        pieces[1],
        pieces[2],
        pieces[3].reshape(CONV, width),
        pieces[4].reshape(D, 2 * H),
        pieces[5],
        pieces[6],
    )


def split_weights(mix_whole, ffn_whole):
    mix_rows = mix_whole.reshape(-1, D)
    ffn_rows = ffn_whole.reshape(-1, D)
    edge = 2 * H * DK + 2 * H * DV
    return (mix_rows[:edge], mix_rows[edge:], ffn_rows[: 2 * FF], ffn_rows[2 * FF :])


PAD = 16
HIGH = dict(precision=HIGHEST, preferred_element_type=jnp.float32)


def mm(a, b):
    return lax.dot_general(a, b, (((1,), (0,)), ((), ())), **HIGH)


def mm_nt(a, b):
    return lax.dot_general(a, b, (((1,), (1,)), ((), ())), **HIGH)


def mm_tn(a, b):
    return lax.dot_general(a, b, (((0,), (0,)), ((), ())), **HIGH)


def halves(a):
    high = a.astype(jnp.bfloat16)
    return high, (a - high.astype(jnp.float32)).astype(jnp.bfloat16)


def wire_mm(a, b, dims):
    high, low = halves(b)
    first = lax.dot_general(a, high, (dims, ((), ())), preferred_element_type=jnp.float32)
    return first + lax.dot_general(a, low, (dims, ((), ())), preferred_element_type=jnp.float32)


def iotas(size):
    shape = (size, size)
    return (
        lax.broadcasted_iota(jnp.int32, shape, 0),
        lax.broadcasted_iota(jnp.int32, shape, 1),
    )


def to_row(column, rows, cols):
    return jnp.sum(jnp.where(rows == cols, column, 0.0), axis=0, keepdims=True)


def unit_inverse(strict_part, rows, cols):
    size = strict_part.shape[0]
    inverse = jnp.where(rows == cols, 1.0, 0.0) - jnp.where(
        (rows // 2 == cols // 2), strict_part, 0.0
    )
    block = 2
    while block < size:
        joined = (rows // (2 * block) == cols // (2 * block)) & (rows // block != cols // block)
        off = jnp.where(joined, strict_part, 0.0)
        inverse = inverse - mm(mm(inverse, off), inverse)
        block = 2 * block
    return inverse


def silu_pair(x):
    gate = jax.nn.sigmoid(x)
    return x * gate, gate * (1.0 + x * (1.0 - gate))


def conv_sum(extended_ref, taps, count):
    total = None
    for tap in range(CONV):
        piece = taps[tap : tap + 1] * extended_ref[pl.ds(8 - (CONV - 1) + tap, count), :]
        total = piece if total is None else total + piece
    return total


def unit_rows(part):
    return lax.rsqrt(jnp.sum(part * part, axis=-1, keepdims=True) + EPSILON)


def decay_terms(decay_column, rows, cols):
    lower = rows >= cols
    size = rows.shape[0]
    spread_in = jnp.broadcast_to(decay_column, (size, 128))
    cumulative = mm(jnp.where(lower, 1.0, 0.0), spread_in)[:, :1]
    across = to_row(cumulative, rows, cols)
    matrix = jnp.where(lower, jnp.exp(jnp.where(lower, cumulative - across, 0.0)), 0.0)
    last = cumulative[size - 1 : size]
    return matrix, jnp.exp(cumulative), jnp.exp(last - cumulative), jnp.exp(last)


def forward_parts(
    projected_ref, border_ref, taps_ref, beta_ref, decay_ref,
    wire_ref, query_ref, keys_ref, values_ref, inverse_ref, extended_ref,
):
    count = projected_ref.shape[0]
    width = taps_ref.shape[1]
    extended_ref[0:8, :] = border_ref[...]
    extended_ref[pl.ds(8, count), :] = projected_ref[:, :width]
    summed = conv_sum(extended_ref, taps_ref[...], count)
    activated = summed * jax.nn.sigmoid(summed)
    rows, cols = iotas(count)
    for head in range(H):
        query_part = activated[:, head * DK : (head + 1) * DK]
        key_part = activated[:, (H + head) * DK : (H + head + 1) * DK]
        start = 2 * H * DK + head * DV
        values = activated[:, start : start + DV]
        query = query_part * unit_rows(query_part) * DK ** (-0.5)
        keys = key_part * unit_rows(key_part)
        beta = beta_ref[:, head : head + 1]
        matrix, grown, to_end, whole = decay_terms(decay_ref[:, head : head + 1], rows, cols)
        system = jnp.where(rows > cols, beta * mm_nt(keys, keys) * matrix, 0.0)
        inverse = unit_inverse(system, rows, cols)
        key_mix = mm(inverse, keys * (beta * grown))
        value_mix = mm(inverse, values * beta)
        base = head * (2 * DK + DV)
        wire_ref[0:count, base : base + DK] = (keys * to_end).astype(jnp.bfloat16)
        wire_ref[0:count, base + DK : base + 2 * DK] = key_mix.astype(jnp.bfloat16)
        wire_ref[0:count, base + 2 * DK : base + 2 * DK + DV] = value_mix.astype(jnp.bfloat16)
        high, low = halves(jnp.broadcast_to(whole, (PAD, 2 * DK + DV)))
        first = lax.broadcasted_iota(jnp.int32, (PAD, 2 * DK + DV), 0) < 8
        tail = jnp.where(first, high.astype(jnp.float32), low.astype(jnp.float32))
        wire_ref[pl.ds(count, PAD), base : base + 2 * DK + DV] = tail.astype(jnp.bfloat16)
        query_ref[:, head * DK : (head + 1) * DK] = query
        keys_ref[:, head * DK : (head + 1) * DK] = keys
        values_ref[:, head * DV : (head + 1) * DV] = values
        inverse_ref[head] = inverse


def wire_parts(wire_ref, index, head, count):
    base = head * (2 * DK + DV)
    to_end = wire_ref[index, 0:count, base : base + DK]
    key_mix = wire_ref[index, 0:count, base + DK : base + 2 * DK]
    value_mix = wire_ref[index, 0:count, base + 2 * DK : base + 2 * DK + DV]
    tail = wire_ref[index, pl.ds(count, PAD), base : base + 128].astype(jnp.float32)
    whole = tail[0:1, 0:1] + tail[8:9, 0:1]
    return to_end, key_mix, value_mix, whole


def own_mix(inverse, keys, values, beta, grown):
    return mm(inverse, keys * (beta * grown)), mm(inverse, values * beta)


def forward_chain(
    place_ref, wire_ref, query_ref, keys_ref, values_ref, inverse_ref, beta_ref, decay_ref,
    gate_ref, gain_ref, head_out_ref, mixed_ref, state_ref, pseudo_ref,
):
    count = query_ref.shape[0]
    state_ref[...] = jnp.zeros_like(state_ref)

    def lap(index, carry):
        for head in range(H):
            to_end, key_mix, value_mix, whole = wire_parts(wire_ref, index, head, count)
            state = state_ref[head]
            pseudo = value_mix.astype(jnp.float32) - wire_mm(key_mix, state, ((1,), (0,)))
            state_ref[head] = whole * state + wire_mm(to_end, pseudo, ((0,), (0,)))
        return carry

    lax.fori_loop(0, place_ref[0], lap, 0)
    rows, cols = iotas(count)
    for head in range(H):
        query = query_ref[:, head * DK : (head + 1) * DK]
        keys = keys_ref[:, head * DK : (head + 1) * DK]
        span = slice(head * DV, (head + 1) * DV)
        beta = beta_ref[:, head : head + 1]
        matrix, grown, to_end, whole = decay_terms(decay_ref[:, head : head + 1], rows, cols)
        key_mix, value_mix = own_mix(inverse_ref[head], keys, values_ref[:, span], beta, grown)
        state = state_ref[head]
        pseudo = value_mix - mm(key_mix, state)
        mixed = mm(query * grown, state) + mm(mm_nt(query, keys) * matrix, pseudo)
        scale = lax.rsqrt(jnp.mean(mixed * mixed, axis=-1, keepdims=True) + EPSILON)
        gated, unused = silu_pair(gate_ref[:, span])
        head_out_ref[:, span] = (mixed * scale * gain_ref[...] * gated).astype(jnp.bfloat16)
        mixed_ref[:, span] = mixed
        pseudo_ref[:, span] = pseudo


def backward_local(
    grad_ref, mixed_ref, query_ref, keys_ref, values_ref, inverse_ref, beta_ref, decay_ref,
    gate_ref, gain_ref, local_ref, grad_mixed_ref, grad_gate_ref, grad_gain_ref,
):
    count = query_ref.shape[0]
    rows, cols = iotas(count)
    gain_total = jnp.zeros((1, DV), jnp.float32)
    for head in range(H):
        query = query_ref[:, head * DK : (head + 1) * DK]
        keys = keys_ref[:, head * DK : (head + 1) * DK]
        span = slice(head * DV, (head + 1) * DV)
        mixed = mixed_ref[:, span]
        grad = grad_ref[:, span]
        scale = lax.rsqrt(jnp.mean(mixed * mixed, axis=-1, keepdims=True) + EPSILON)
        plain = mixed * scale
        gated, slope = silu_pair(gate_ref[:, span])
        grad_gate_ref[:, span] = grad * plain * gain_ref[...] * slope
        grad_normed = grad * gated
        gain_total = gain_total + jnp.sum(grad_normed * plain, axis=0, keepdims=True)
        pulled = grad_normed * gain_ref[...]
        grad_mixed = scale * (pulled - plain * jnp.mean(pulled * plain, axis=-1, keepdims=True))
        grad_mixed_ref[:, span] = grad_mixed
        beta = beta_ref[:, head : head + 1]
        matrix, grown, to_end, whole = decay_terms(decay_ref[:, head : head + 1], rows, cols)
        key_mix = mm(inverse_ref[head], keys * (beta * grown))
        grad_pseudo = mm_tn(mm_nt(query, keys) * matrix, grad_mixed)
        local = mm_tn(query * grown, grad_mixed) - mm_tn(key_mix, grad_pseudo)
        local_ref[head * DK : (head + 1) * DK, :] = local.astype(jnp.bfloat16)
    grad_gain_ref[...] = gain_total


def backward_chain(
    place_ref, wire_ref, local_ref, query_ref, keys_ref, values_ref, inverse_ref, beta_ref,
    decay_ref, state_ref, pseudo_ref, grad_mixed_ref, projected_ref, border_ref, taps_ref,
    grad_conv_ref, grad_border_ref, grad_taps_ref, grad_beta_ref, grad_decay_ref,
    after_ref, extended_ref, padded_ref,
):
    count = query_ref.shape[0]
    width = taps_ref.shape[1]
    devices = wire_ref.shape[0]
    after_ref[...] = jnp.zeros_like(after_ref)

    def lap(step, carry):
        index = devices - 1 - step
        for head in range(H):
            to_end, key_mix, value_mix, whole = wire_parts(wire_ref, index, head, count)
            after = after_ref[head]
            inner = wire_mm(to_end, after, ((1,), (0,)))
            local = local_ref[index, head * DK : (head + 1) * DK, :].astype(jnp.float32)
            after_ref[head] = whole * after - wire_mm(key_mix, inner, ((0,), (0,))) + local
        return carry

    lax.fori_loop(0, devices - 1 - place_ref[0], lap, 0)
    extended_ref[0:8, :] = border_ref[...]
    extended_ref[pl.ds(8, count), :] = projected_ref[:, :width]
    taps = taps_ref[...]
    summed = conv_sum(extended_ref, taps, count)
    activated, slope = silu_pair(summed)
    padded_ref[0:8, :] = jnp.zeros((8, width), jnp.float32)
    padded_ref[pl.ds(8 + count, 8), :] = jnp.zeros((8, width), jnp.float32)
    rows, cols = iotas(count)
    lower = rows >= cols
    strict = rows > cols
    lanes = lax.broadcasted_iota(jnp.int32, (count, 128), 1)
    beta_out = jnp.zeros((count, 128), jnp.float32)
    cumulative_out = jnp.zeros((count, 128), jnp.float32)
    row_column = lax.broadcasted_iota(jnp.int32, (count, 1), 0)
    for head in range(H):
        query = query_ref[:, head * DK : (head + 1) * DK]
        keys = keys_ref[:, head * DK : (head + 1) * DK]
        span = slice(head * DV, (head + 1) * DV)
        values = values_ref[:, span]
        beta = beta_ref[:, head : head + 1]
        matrix, grown, to_end, whole = decay_terms(decay_ref[:, head : head + 1], rows, cols)
        inverse = inverse_ref[head]
        state = state_ref[head]
        after = after_ref[head]
        pseudo = pseudo_ref[:, span]
        grad_mixed = grad_mixed_ref[:, span]
        keys_grown = keys * (beta * grown)
        key_mix = mm(inverse, keys_grown)
        value_mix = mm(inverse, values * beta)
        gram = mm_nt(keys, keys)
        system = jnp.where(strict, beta * gram * matrix, 0.0)
        scores = mm_nt(query, keys) * matrix
        keys_end = keys * to_end
        query_grown = query * grown
        grad_query_grown = mm_nt(grad_mixed, state)
        grad_scores = jnp.where(lower, mm_nt(grad_mixed, pseudo), 0.0)
        grad_pseudo = mm_tn(scores, grad_mixed) + mm(keys_end, after)
        grad_keys_end = mm_nt(pseudo, after)
        grad_whole = jnp.sum(jnp.sum(after * state, axis=1, keepdims=True), axis=0, keepdims=True)
        grad_value_in = mm_tn(inverse, grad_pseudo)
        grad_key_in = mm_tn(inverse, -mm_nt(grad_pseudo, state))
        grad_system = -jnp.where(
            strict, mm_nt(grad_value_in, value_mix) + mm_nt(grad_key_in, key_mix), 0.0
        )
        grad_raw = grad_scores * matrix
        grad_query = mm(grad_raw, keys) + grad_query_grown * grown
        grad_keys = mm_tn(grad_raw, query)
        weighted = grad_system * matrix
        grad_beta = jnp.sum(weighted * gram, axis=1, keepdims=True)
        grad_gram = weighted * beta
        grad_keys = grad_keys + mm(grad_gram, keys) + mm_tn(grad_gram, keys)
        spread = grad_scores * scores + grad_system * system
        grad_cumulative = jnp.sum(spread, axis=1, keepdims=True)
        across = jnp.sum(spread, axis=0, keepdims=True)
        grad_cumulative = grad_cumulative - jnp.sum(
            jnp.where(rows == cols, across, 0.0), axis=1, keepdims=True
        )
        grad_keys = grad_keys + grad_key_in * (beta * grown)
        through = jnp.sum(grad_key_in * keys, axis=1, keepdims=True) * grown
        grad_beta = grad_beta + through + jnp.sum(grad_value_in * values, axis=1, keepdims=True)
        grad_cumulative = grad_cumulative + through * beta
        grad_values = grad_value_in * beta
        grad_cumulative = grad_cumulative + jnp.sum(
            grad_query_grown * query_grown, axis=1, keepdims=True
        )
        grad_keys = grad_keys + grad_keys_end * to_end
        ending = jnp.sum(grad_keys_end * keys_end, axis=1, keepdims=True)
        final = jnp.sum(ending, axis=0, keepdims=True) + whole * grad_whole
        grad_cumulative = grad_cumulative - ending + jnp.where(row_column == count - 1, final, 0.0)
        beta_out = jnp.where(lanes == head, grad_beta, beta_out)
        cumulative_out = jnp.where(lanes == head, grad_cumulative, cumulative_out)
        key_part = activated[:, (H + head) * DK : (H + head + 1) * DK]
        key_scale = unit_rows(key_part)
        query_part = activated[:, head * DK : (head + 1) * DK]
        query_scale = unit_rows(query_part)
        factor = DK ** (-0.5)
        grad_query_part = (factor * query_scale) * (
            grad_query
            - query_part
            * (query_scale * query_scale)
            * jnp.sum(grad_query * query_part, axis=-1, keepdims=True)
        )
        grad_key_part = key_scale * (
            grad_keys
            - key_part
            * (key_scale * key_scale)
            * jnp.sum(grad_keys * key_part, axis=-1, keepdims=True)
        )
        spots = (head * DK, (H + head) * DK, 2 * H * DK + head * DV)
        for spot, grad in zip(spots, (grad_query_part, grad_key_part, grad_values)):
            size = grad.shape[1]
            padded_ref[pl.ds(8, count), spot : spot + size] = grad * slope[:, spot : spot + size]
    grad_beta_ref[...] = beta_out
    grad_decay_ref[...] = mm_tn(jnp.where(lower, 1.0, 0.0), cumulative_out)
    conv_total = jnp.zeros((count, width), jnp.float32)
    border_total = jnp.zeros((8, width), jnp.float32)
    summed_grad = padded_ref[pl.ds(8, count), :]
    tap_rows = lax.broadcasted_iota(jnp.int32, (8, width), 0)
    taps_total = jnp.zeros((8, width), jnp.float32)
    for tap in range(CONV):
        shift = CONV - 1 - tap
        conv_total = conv_total + taps[tap : tap + 1] * padded_ref[pl.ds(8 + shift, count), :]
        border_total = border_total + taps[tap : tap + 1] * padded_ref[pl.ds(shift, 8), :]
        piece = jnp.sum(
            summed_grad * extended_ref[pl.ds(8 - (CONV - 1) + tap, count), :],
            axis=0,
            keepdims=True,
        )
        taps_total = jnp.where(tap_rows == tap, piece, taps_total)
    grad_conv_ref[...] = conv_total
    grad_border_ref[...] = border_total
    grad_taps_ref[...] = taps_total


def fused(body, outputs, scratch=(), scalars=0, cost=(0, 0), label=None):
    def call(*args):
        vmem = pl.BlockSpec(memory_space=pltpu.VMEM)
        smem = pl.BlockSpec(memory_space=pltpu.SMEM)
        return pl.pallas_call(
            body,
            out_shape=outputs,
            in_specs=[smem] * scalars + [vmem] * (len(args) - scalars),
            out_specs=[vmem] * len(outputs),
            scratch_shapes=list(scratch),
            compiler_params=pltpu.CompilerParams(vmem_limit_bytes=60 * 2**20),
            cost_estimate=pl.CostEstimate(
                flops=cost[0], bytes_accessed=cost[1], transcendentals=0
            ),
            name=label,
        )(*args)

    return call


def gates(gate_logits, a_log, dt_bias):
    beta = jax.nn.sigmoid(gate_logits[:, :H])
    decay = -jnp.exp(a_log) * jax.nn.softplus(gate_logits[:, H:] + dt_bias)
    return beta, decay


def scatter_rows(pieces):
    outer, inner = lax.axis_size("dp"), lax.axis_size("ctx")
    whole = jnp.concatenate([piece.astype(jnp.bfloat16) for piece in pieces], axis=0)
    lane = math.gcd(whole.size // (outer * inner), D)
    blocks = whole.reshape(outer, inner, -1, lane)
    part = lax.psum_scatter(blocks, "ctx", scatter_dimension=1, tiled=False)
    own = lax.psum_scatter(part, "dp", scatter_dimension=0, tiled=False)
    return own.astype(jnp.float32).reshape(-1)


def adam_step(weight, grad_full, first, second, clip):
    grad_clipped = grad_full * clip
    first_new = BETA_ONE * first + (1.0 - BETA_ONE) * grad_clipped
    second_new = BETA_TWO * second + (1.0 - BETA_TWO) * grad_clipped * grad_clipped
    update = (
        first_new / CORRECT_ONE / (jnp.sqrt(second_new / CORRECT_TWO) + ADAM_EPS)
        + DECAY_RATE * weight
    )
    return (weight - LEARN_RATE * update, first_new, second_new)


def body(
    inputs,
    cotangent,
    mixer_params,
    mixer_first,
    mixer_second,
    ffn_params,
    ffn_first,
    ffn_second,
    small_params,
    small_first,
    small_second,
):
    gain_one, gain_two, gain_head, tap_values, w_gates, a_log, dt_bias = unpack_small(small_params)
    width = tap_values.shape[1]
    mix_part = mixer_params.astype(jnp.bfloat16)
    ffn_part = ffn_params.astype(jnp.bfloat16)
    mix_whole, ffn_whole = (
        lax.all_gather(mix_part, ("dp", "ctx"), axis=0, tiled=True),
        lax.all_gather(ffn_part, ("dp", "ctx"), axis=0, tiled=True),
    )
    w_in, w_out, w_ffn, w_down = split_weights(mix_whole, ffn_whole)
    x_float = inputs[0].astype(jnp.float32)
    count = x_float.shape[0]
    normed_in = norm_scale(x_float, gain_one).astype(jnp.bfloat16)
    projected = jnp.dot(normed_in, w_in.T, preferred_element_type=jnp.float32)
    gate_logits = jnp.dot(normed_in.astype(jnp.float32), w_gates, precision=HIGHEST)
    f32 = jnp.float32
    devices = lax.axis_size("ctx")
    place = lax.axis_index("ctx").astype(jnp.int32).reshape(1)
    out_gate = projected[:, width:]
    edge = from_behind(projected[count - 8 :, :width], "ctx", 1)
    border = jnp.where(lax.broadcasted_iota(jnp.int32, (8, 1), 0) >= 8 - (CONV - 1), edge, 0.0)
    (beta, decay), pull_gates = jax.vjp(gates, gate_logits, a_log, dt_bias)
    wire, query, keys, values, inverse = fused(
        forward_parts,
        (
            jax.ShapeDtypeStruct((count + PAD, H * (2 * DK + DV)), jnp.bfloat16),
            jax.ShapeDtypeStruct((count, H * DK), f32),
            jax.ShapeDtypeStruct((count, H * DK), f32),
            jax.ShapeDtypeStruct((count, H * DV), f32),
            jax.ShapeDtypeStruct((H, count, count), f32),
        ),
        scratch=(pltpu.VMEM((count + 8, width), f32),),
        label="forward_parts",
    )(projected, border, tap_values, beta, decay)
    wires = lax.all_gather(wire, "ctx")
    gain_row = gain_head.reshape(1, DV)
    head_out, mixed, state, pseudo = fused(
        forward_chain,
        (
            jax.ShapeDtypeStruct((count, H * DV), jnp.bfloat16),
            jax.ShapeDtypeStruct((count, H * DV), f32),
            jax.ShapeDtypeStruct((H, DK, DV), f32),
            jax.ShapeDtypeStruct((count, H * DV), f32),
        ),
        scalars=1,
        label="forward_chain",
    )(place, wires, query, keys, values, inverse, beta, decay, out_gate, gain_row)
    resid = x_float + jnp.dot(head_out, w_out, preferred_element_type=jnp.float32)
    normed_mid = norm_scale(resid, gain_two).astype(jnp.bfloat16)
    ffn_pre = jnp.dot(normed_mid, w_ffn.T, preferred_element_type=jnp.float32)
    gate_part = ffn_pre[:, :FF]
    up_part = ffn_pre[:, FF:]
    hidden_act = swiglu(gate_part, up_part).astype(jnp.bfloat16)
    result = (resid + jnp.dot(hidden_act, w_down, preferred_element_type=jnp.float32)).astype(
        jnp.bfloat16
    )
    seq_grad = cotangent[0]
    grad_float = seq_grad.astype(jnp.float32)
    grad_down = jnp.dot(hidden_act.T, seq_grad, preferred_element_type=jnp.float32)
    grad_hidden = jnp.dot(seq_grad, w_down.T, preferred_element_type=jnp.float32)
    unused_one, pull_swiglu = jax.vjp(swiglu, gate_part, up_part)
    grad_gate, grad_up = pull_swiglu(grad_hidden)
    grad_pre = jnp.concatenate([grad_gate, grad_up], axis=1).astype(jnp.bfloat16)
    grad_ffn = jnp.dot(grad_pre.T, normed_mid, preferred_element_type=jnp.float32)
    grad_mid = jnp.dot(grad_pre, w_ffn, preferred_element_type=jnp.float32)
    unused_two, pull_mid = jax.vjp(norm_scale, resid, gain_two)
    grad_through, grad_gain_two = pull_mid(grad_mid)
    grad_resid = grad_float + grad_through
    resid_half = grad_resid.astype(jnp.bfloat16)
    grad_out = jnp.dot(head_out.T, resid_half, preferred_element_type=jnp.float32)
    grad_head = jnp.dot(resid_half, w_out.T, preferred_element_type=jnp.float32)
    local, grad_mixed, grad_gate_out, grad_gain_head = fused(
        backward_local,
        (
            jax.ShapeDtypeStruct((H * DK, DV), jnp.bfloat16),
            jax.ShapeDtypeStruct((count, H * DV), f32),
            jax.ShapeDtypeStruct((count, H * DV), f32),
            jax.ShapeDtypeStruct((1, DV), f32),
        ),
        label="backward_local",
    )(grad_head, mixed, query, keys, values, inverse, beta, decay, out_gate, gain_row)
    locals_all = lax.all_gather(local, "ctx")
    locals_all, grad_ffn, grad_down = lax.optimization_barrier((locals_all, grad_ffn, grad_down))
    ffn_shard = scatter_rows((grad_ffn, grad_down))
    grad_conv, grad_border, grad_taps, grad_beta, grad_decay = fused(
        backward_chain,
        (
            jax.ShapeDtypeStruct((count, width), f32),
            jax.ShapeDtypeStruct((8, width), f32),
            jax.ShapeDtypeStruct((8, width), f32),
            jax.ShapeDtypeStruct((count, 128), f32),
            jax.ShapeDtypeStruct((count, 128), f32),
        ),
        scratch=(
            pltpu.VMEM((H, DK, DV), f32),
            pltpu.VMEM((count + 8, width), f32),
            pltpu.VMEM((count + 16, width), f32),
        ),
        scalars=1,
        label="backward_chain",
    )(
        place, wires, locals_all, query, keys, values, inverse, beta, decay, state, pseudo,
        grad_mixed, projected, border, tap_values,
    )
    grad_logits, grad_alog, grad_bias = pull_gates((grad_beta[:, :H], grad_decay[:, :H]))
    returned = from_behind(grad_border, "ctx", -1)[8 - (CONV - 1) :]
    grad_conv = grad_conv.at[count - (CONV - 1) :].add(returned)
    grad_proj = jnp.concatenate([grad_conv, grad_gate_out], axis=1).astype(jnp.bfloat16)
    grad_in = jnp.dot(grad_proj.T, normed_in, preferred_element_type=jnp.float32)
    grad_normed = jnp.dot(grad_proj, w_in, preferred_element_type=jnp.float32) + jnp.dot(
        grad_logits, w_gates.T, precision=HIGHEST
    )
    grad_gates = jnp.dot(normed_in.astype(jnp.float32).T, grad_logits, precision=HIGHEST)
    unused_six, pull_in = jax.vjp(norm_scale, x_float, gain_one)
    grad_x, grad_gain_one = pull_in(grad_normed)
    grad_input = (grad_resid + grad_x).astype(jnp.bfloat16)
    small_local = jnp.concatenate(
        [
            grad_gain_one,
            grad_gain_two,
            grad_gain_head.reshape(-1),
            grad_taps[:CONV].reshape(-1),
            grad_gates.reshape(-1),
            grad_alog,
            grad_bias,
        ]
    )
    small_grad = lax.psum(small_local, ("dp", "ctx"))
    ffn_shard, grad_in, grad_out = lax.optimization_barrier((ffn_shard, grad_in, grad_out))
    mix_shard = scatter_rows((grad_in, grad_out))
    small_grad, mix_shard = lax.optimization_barrier((small_grad, mix_shard))
    shard_squares = jnp.sum(mix_shard * mix_shard) + jnp.sum(ffn_shard * ffn_shard)
    total_squares = lax.psum(shard_squares, ("dp", "ctx"))
    squares = total_squares + jnp.sum(small_grad * small_grad)
    clip = jnp.minimum(1.0, MAX_NORM / (jnp.sqrt(squares) + 1e-06))
    mixer_new, mixer_first_new, mixer_second_new = adam_step(
        mixer_params, mix_shard, mixer_first, mixer_second, clip
    )
    ffn_new, ffn_first_new, ffn_second_new = adam_step(
        ffn_params, ffn_shard, ffn_first, ffn_second, clip
    )
    small_new, small_first_new, small_second_new = adam_step(
        small_params, small_grad, small_first, small_second, clip
    )
    return (
        result[None],
        grad_input[None],
        mix_shard,
        ffn_shard,
        small_grad,
        mixer_new,
        mixer_first_new,
        mixer_second_new,
        ffn_new,
        ffn_first_new,
        ffn_second_new,
        small_new,
        small_first_new,
        small_second_new,
    )


def solution(mesh):
    return jax.shard_map(
        body,
        mesh=mesh,
        in_specs=(
            P("dp", "ctx", None),
            P("dp", "ctx", None),
            P(("dp", "ctx")),
            P(("dp", "ctx")),
            P(("dp", "ctx")),
            P(("dp", "ctx")),
            P(("dp", "ctx")),
            P(("dp", "ctx")),
            P(),
            P(),
            P(),
        ),
        out_specs=(
            P("dp", "ctx", None),
            P("dp", "ctx", None),
            P(("dp", "ctx")),
            P(("dp", "ctx")),
            P(),
            P(("dp", "ctx")),
            P(("dp", "ctx")),
            P(("dp", "ctx")),
            P(("dp", "ctx")),
            P(("dp", "ctx")),
            P(("dp", "ctx")),
            P(),
            P(),
            P(),
        ),
        check_vma=False,
    )
```
